32 devices in a mesh: groups: 2 (over x), seq: 8 (over z, y), pipe: 2 (over core).
Axes of the slice: x: 2, y: 2, z: 4, core: 2. Of those that a mesh axis runs over, the one named last changes fastest.
Arguments:
- tokens: bfloat16 [2, 2048, 1440], P('pipe', ('groups', 'seq')), parts along dimension 1, may hold values from -6 to 6
- routes: int32 [2, 2048, 4], P('pipe', ('groups', 'seq')), parts along dimension 1, may hold values from 0 to 15, all different within a row; in each aligned block of 128 rows (0 to 127, 128 to 255, ..., all dimensions but the last counted through in order) at most 48 rows name the same one
- route_weights: float32 [2, 2048, 4], P('pipe', ('groups', 'seq')), parts along dimension 1, may hold values from 0.1 to 1
- moe_gain: float32 [1440], replicated, may hold values from 0.5 to 1.5
- gate_up: bfloat16 [32, 1440, 1440], P('seq'), may hold values from -0.15625 to 0.15625
- down_proj: bfloat16 [32, 720, 1440], P('seq'), may hold values from -0.15625 to 0.15625
- attn_gain: float32 [1440], replicated, may hold values from 0.5 to 1.5
- qkv_proj: bfloat16 [1440, 2560], P('seq'), may hold values from -0.15625 to 0.15625
- head_sink_logits: float32 [32], replicated, may hold values from 3 to 6
- out_proj: bfloat16 [2048, 1440], P('seq'), may hold values from -0.125 to 0.125
Outputs:
- layer_output: bfloat16 [2, 2048, 1440], P('pipe', ('groups', 'seq')), parts along dimension 1
The draws below stay inside these ranges and needn't reach their ends.
There are 2 independent parts, one for each index of `groups`. The reference program is written for one: setup_inputs(seed, part) draws one part's arguments, and reference() takes and returns one part's arrays. A program takes and returns all parts, laid end to end along the dimension named above; an argument that names none is the same for every part. Nothing has to cross between parts.
Inputs may be any that keep to these rules, and one draw needn't show every extreme that they name: `routes`: within the 128 positions of one micro-batch on one index of seq, a token names each of its 4 experts once, and each expert is named by at most 48 tokens; one expert is named by exactly 48 of them.
All inputs are finite; a program needn't handle non-finite values.
Results may differ from the reference program's by a relative error of at most 0.0085.
Values may be sent and summed in bfloat16 or wider, within the bound.
A program may use at most 128 MiB of HBM per device.

```python
import math
import jax
import jax.numpy as jnp
import numpy as np
from jax import lax

D = 1440
E = 16
H = 1440
TOP = 4
QUERY_HEADS = 32
KEY_VALUE_HEADS = 4
HEAD_SIZE = 64
WINDOW_SPAN = 128
TOK_DEV = 128
HALF = 720
SLABS = 32
CAP = 48
MB = 2
TOKENS = 1024
QKV = 2560
N_SEQ = 8


def shard_levels(stream_key, extent, shards, least, top_value):
    def one(position, shards_of):
        steps = jax.random.uniform(jax.random.fold_in(jax.random.fold_in(stream_key, 6), position), (shards_of,), jnp.float32, least / len(shards), top_value / len(shards))
        return jnp.repeat(jnp.exp(steps), extent[position] // shards_of).reshape((-1,) + (1,) * (len(extent) - position - 1))

    loudness = one(*shards[0])
    for cut in shards[1:]:
        loudness = loudness * one(*cut)
    return loudness


def deal_out(key, own, number, rows, amount, top, most, lean):
    sequence = jax.random.permutation(key, amount)
    packed, usual = load_shares(amount, rows * top, most, lean, True), load_shares(amount, rows * top, most, lean, False)
    places = jnp.arange(amount)

    def named(sizes, rotation):
        used = int((sizes > 0).sum())
        fixed = max(1, used // 4)
        moved = fixed + (places - fixed + rotation * (used - fixed)) % max(1, amount - fixed)
        return jnp.zeros((amount,), jnp.int32).at[sequence[jnp.where(places < fixed, places, moved)]].set(jnp.asarray(sizes, jnp.int32))

    sizes = jnp.where(number % 4 == 0, named(packed, number // 4), named(usual, number - number // 4 - 1))
    mixed = jax.random.permutation(jax.random.fold_in(own, 3), amount)
    source_of, sink = mixed[0:amount // 2 * 2:2], mixed[1:amount // 2 * 2:2]
    slack = jnp.minimum(sizes[source_of] - 1, most - sizes[sink]) // 2
    slack = jnp.where((source_of == sequence[0]) | (sink == sequence[0]) | (sizes[sink] == 0), 0, jnp.maximum(slack, 0))
    moved = jax.random.randint(jax.random.fold_in(own, 4), (amount // 2,), 0, 1 << 20) % (slack + 1)
    sizes = sizes.at[source_of].add(-moved).at[sink].add(moved)
    items = jnp.searchsorted(jnp.cumsum(sizes), jnp.arange(rows * top), side="right").astype(jnp.int32)
    grid = items.reshape(top, rows).T
    grid = grid[jax.random.permutation(jax.random.fold_in(own, 1), rows)]
    rotation = jax.random.randint(jax.random.fold_in(own, 2), (rows, 1), 0, top)
    return jnp.take_along_axis(grid, (jnp.arange(top)[None, :] + rotation) % top, axis=1)


def load_shares(amount, total, bound, slope, full):
    loads = [(1 << 20) // math.isqrt(grade ** slope) + 1 for grade in range(1, amount + 1)]
    largest = bound if full else min(bound, max(-(-total // amount), total * loads[0] // sum(loads)))
    least = 1 if total - largest >= amount - 1 else 0
    counts, spare = [largest] + [least] * (amount - 1), total - largest - least * (amount - 1)
    while spare > 0:
        free = [i for i in range(1, amount) if counts[i] < largest] or [i for i in range(1, amount) if counts[i] < bound]
        pool, remaining = sum([loads[i] for i in free]), spare
        for i in free:
            addition = min(bound - counts[i], max(1, remaining * loads[i] // pool), spare)
            counts[i] = counts[i] + addition
            spare = spare - addition
    return np.array(counts)


def centred(rng, dims, width, most, shards=(), kind=jnp.bfloat16):
    loudness = shard_levels(rng, dims, shards, -0.22, 0.18) if shards else 1.0
    entries = jax.random.normal(rng, dims, jnp.float32) * width * loudness
    return jnp.minimum(jnp.maximum(entries, -most), most).astype(kind)


def setup_inputs(seed: int = 0, part: int = 0) -> dict:
    keys = jax.random.split(jax.random.key(seed), 11)
    own_keys = jax.random.split(jax.random.fold_in(keys[10], part), 11)
    tokens = centred(own_keys[0], (MB, TOKENS, D), 1.0, 6.0, ((0, 2), (1, 8)))
    routes_keys = jax.random.split(jax.random.fold_in(own_keys[1], 1), MB * TOKENS // TOK_DEV)
    routes_turns = jax.random.permutation(jax.random.fold_in(own_keys[1], 3), MB * TOKENS // TOK_DEV)
    routes = jax.vmap(lambda own, number: deal_out(jax.random.fold_in(own_keys[1], 2), own, number, TOK_DEV, E, TOP, CAP, 2))(routes_keys, routes_turns).reshape((MB, TOKENS, TOP))
    route_weights = jnp.clip(0.1 + 0.9 * jax.random.uniform(own_keys[2], (MB, TOKENS, TOP), jnp.float32) ** shard_levels(own_keys[2], (MB, TOKENS, TOP), ((0, 2), (1, 8)), -0.2, 0.2), 0.1, 1.0)
    moe_gain = jnp.clip(1.0 + 0.1 * jax.random.normal(keys[3], (D,), jnp.float32), 0.5, 1.5)
    gate_up = centred(keys[4], (SLABS, D, 2 * HALF), D ** -0.5, 0.15625, ((0, 8),))
    down_proj = centred(keys[5], (SLABS, HALF, D), H ** -0.5, 0.15625, ((0, 8),))
    attn_gain = jnp.clip(1.0 + 0.1 * jax.random.normal(keys[6], (D,), jnp.float32), 0.5, 1.5)
    qkv_proj = centred(keys[7], (D, QKV), D ** -0.5, 0.15625, ((0, 8),))
    head_sink_logits = jnp.clip(jax.random.uniform(keys[8], (QUERY_HEADS,), jnp.float32, 3.0, 6.0), 3.0, 6.0)
    out_proj = centred(keys[9], (QUERY_HEADS * HEAD_SIZE, D), (QUERY_HEADS * HEAD_SIZE) ** -0.5, 0.125, ((0, 8),))
    return {"tokens": tokens, "routes": routes, "route_weights": route_weights, "moe_gain": moe_gain, "gate_up": gate_up, "down_proj": down_proj, "attn_gain": attn_gain, "qkv_proj": qkv_proj, "head_sink_logits": head_sink_logits, "out_proj": out_proj}


eps = 1e-05

def rms_scale(value_matrix, gain):
    widened = value_matrix.astype(jnp.float32)
    mean_square = lax.optimization_barrier(jnp.mean(widened * widened, axis=-1, keepdims=True))
    return (widened * lax.rsqrt(mean_square + eps) * gain).astype(jnp.bfloat16)

def slot_positions(route_rows):
    flat = route_rows.reshape(-1).astype(jnp.int32)
    onehot = (flat[:, None] == jnp.arange(E, dtype=jnp.int32)[None, :]).astype(jnp.int32)
    earlier = jnp.cumsum(onehot, axis=0) - onehot
    return (flat * CAP + lax.optimization_barrier(jnp.sum(earlier * onehot, axis=1))).astype(jnp.int32)

def expert_apply(items):
    rows, pair_gate_up, pair_down = items
    gate_matrix = jnp.concatenate([pair_gate_up[0][:, :HALF], pair_gate_up[1][:, :HALF]], axis=1)
    up_matrix = jnp.concatenate([pair_gate_up[0][:, HALF:], pair_gate_up[1][:, HALF:]], axis=1)
    down_matrix = jnp.concatenate([pair_down[0], pair_down[1]], axis=0)
    gate = jnp.dot(rows, gate_matrix, preferred_element_type=jnp.float32)
    upper = jnp.dot(rows, up_matrix, preferred_element_type=jnp.float32)
    hidden = (gate * jax.nn.sigmoid(1.702 * gate) * (upper + 1.0)).astype(jnp.bfloat16)
    return jnp.dot(hidden, down_matrix, preferred_element_type=jnp.float32).astype(jnp.bfloat16)

def dispatch_block(items):
    rows, route_rows = items
    positions = slot_positions(route_rows)
    source = jnp.repeat(rows, TOP, axis=0)
    table = jnp.zeros((E * CAP, D), jnp.bfloat16).at[positions].set(source)
    return (table, positions)

def pick_rows(results, positions):
    return results[positions]

def moe_block(tokens_mb, routes_mb, weights_mb, moe_gain, gate_up, down_proj):
    normed = rms_scale(tokens_mb, moe_gain)
    blocks = normed.reshape(N_SEQ, TOK_DEV, D)
    route_blocks = routes_mb.reshape(N_SEQ, TOK_DEV, TOP)
    tables, positions = lax.map(dispatch_block, (blocks, route_blocks))
    per_expert = tables.reshape(N_SEQ, E, CAP, D).transpose(1, 0, 2, 3).reshape(E, N_SEQ * CAP, D)
    results = lax.map(expert_apply, (per_expert, gate_up.reshape(E, 2, D, 2 * HALF), down_proj.reshape(E, 2, HALF, D)))
    results = results.reshape(E, N_SEQ, CAP, D).transpose(1, 0, 2, 3).reshape(N_SEQ, E * CAP, D)
    picked = jax.vmap(pick_rows)(results, positions)
    picked = picked.reshape(TOKENS, TOP, D).astype(jnp.float32)
    summed = tokens_mb.astype(jnp.float32) + lax.optimization_barrier(jnp.sum(picked * weights_mb[:, :, None], axis=1))
    return summed.astype(jnp.bfloat16)

def attention_all(hidden_all, attn_gain, qkv_proj, head_sink_logits, out_proj):
    length = hidden_all.shape[0]
    query_groups = QUERY_HEADS // KEY_VALUE_HEADS
    normed = rms_scale(hidden_all, attn_gain)
    packed_heads = lax.optimization_barrier(jnp.dot(normed, qkv_proj, preferred_element_type=jnp.float32).astype(jnp.bfloat16)).astype(jnp.float32)
    query_matrix = packed_heads[:, :QUERY_HEADS * HEAD_SIZE]
    key_matrix = packed_heads[:, QUERY_HEADS * HEAD_SIZE:(QUERY_HEADS + KEY_VALUE_HEADS) * HEAD_SIZE]
    value_matrix = packed_heads[:, (QUERY_HEADS + KEY_VALUE_HEADS) * HEAD_SIZE:]
    padding_rows = jnp.zeros((WINDOW_SPAN, KEY_VALUE_HEADS * HEAD_SIZE), jnp.float32)
    keys_extended = jnp.concatenate([padding_rows, key_matrix], axis=0)
    values_extended = jnp.concatenate([padding_rows, value_matrix], axis=0)
    scale = float(HEAD_SIZE) ** (-0.5)
    sink_mass_total = jnp.exp(head_sink_logits).reshape(KEY_VALUE_HEADS, query_groups, 1, 1)

    def one_block(index):
        start_position = (index * WINDOW_SPAN).astype(jnp.int32)
        rows_of_queries = lax.dynamic_slice_in_dim(query_matrix, start_position, WINDOW_SPAN, 0).reshape(WINDOW_SPAN, KEY_VALUE_HEADS, query_groups, HEAD_SIZE)
        rows_of_keys = lax.dynamic_slice_in_dim(keys_extended, start_position, 2 * WINDOW_SPAN, 0).reshape(2 * WINDOW_SPAN, KEY_VALUE_HEADS, HEAD_SIZE)
        rows_of_values = lax.dynamic_slice_in_dim(values_extended, start_position, 2 * WINDOW_SPAN, 0).reshape(2 * WINDOW_SPAN, KEY_VALUE_HEADS, HEAD_SIZE)
        scores = jnp.einsum('qhgd,khd->hgqk', rows_of_queries, rows_of_keys) * scale
        query_pos = start_position + jnp.arange(WINDOW_SPAN, dtype=jnp.int32)
        key_pos = start_position - WINDOW_SPAN + jnp.arange(2 * WINDOW_SPAN, dtype=jnp.int32)
        distance = query_pos[:, None] - key_pos[None, :]
        allowed = (distance >= 0) & (distance < WINDOW_SPAN) & (key_pos[None, :] >= 0)
        weights = jnp.where(allowed, jnp.exp(scores), 0.0)
        total = lax.optimization_barrier(jnp.sum(weights, axis=-1, keepdims=True)) + sink_mass_total
        probs = lax.optimization_barrier((weights / total).astype(jnp.bfloat16)).astype(jnp.float32)
        mixed = jnp.einsum('hgqk,khd->qhgd', probs, rows_of_values)
        return mixed.reshape(WINDOW_SPAN, QUERY_HEADS * HEAD_SIZE).astype(jnp.bfloat16)
    attended = lax.map(one_block, jnp.arange(length // WINDOW_SPAN, dtype=jnp.int32)).reshape(length, QUERY_HEADS * HEAD_SIZE)
    projected = jnp.dot(attended, out_proj, preferred_element_type=jnp.float32)
    return (hidden_all.astype(jnp.float32) + projected).astype(jnp.bfloat16)

def reference(tokens, routes, route_weights, moe_gain, gate_up, down_proj, attn_gain, qkv_proj, head_sink_logits, out_proj):
    sections = []
    for index in range(MB):
        sections.append(moe_block(tokens[index], routes[index], route_weights[index], moe_gain, gate_up, down_proj))
    whole = jnp.stack(sections).reshape(MB * TOKENS, D)
    result = attention_all(whole, attn_gain, qkv_proj, head_sink_logits, out_proj)
    return result.reshape(MB, TOKENS, D)
```

```python
import functools

import jax
import jax.numpy as jnp
from jax import lax
from jax.experimental import pallas as pl
from jax.experimental.pallas import tpu as pltpu
from jax.sharding import PartitionSpec as P

MESH = pl.DeviceIdType.MESH
E = 16
TOP = 4
QUERY_HEADS = 32
KEY_VALUE_HEADS = 4
HEAD_SIZE = 64
WINDOW_SPAN = 128
HALF = 720
CAP = 48


eps = 1e-05


def from_partner(value, axis, distance):
    return lax.ppermute(value, axis, [(i, i ^ 1 << distance) for i in range(lax.axis_size(axis))])


def shifted(value, axis, steps):
    count = lax.axis_size(axis)
    pairs = [(source, (source + steps) % count) for source in range(count)]
    return lax.ppermute(value, axis, pairs)


def passed_along(value, axis, steps):
    count = lax.axis_size(axis)
    first, last = (max(0, -steps), min(count, count - steps))
    return lax.ppermute(value, axis, [(source, source + steps) for source in range(first, last)])


def rms_scale(value_matrix, gain):
    widened = value_matrix.astype(jnp.float32)
    mean_square = jnp.mean(widened * widened, axis=-1, keepdims=True)
    return (widened * lax.rsqrt(mean_square + eps) * gain).astype(jnp.bfloat16)


def slot_positions(route_rows):
    flat = route_rows.reshape(-1)
    onehot = (flat[:, None] == jnp.arange(E, dtype=jnp.int32)[None, :]).astype(jnp.int32)
    earlier = jnp.cumsum(onehot, axis=0) - onehot
    return flat * CAP + jnp.sum(earlier * onehot, axis=1)


def expert_layer(local, route_rows, route_scale, moe_gain, gate_up, down_proj):
    tok_count, width = local.shape
    seq_count = lax.axis_size("seq")
    per_device = gate_up.shape[0]
    normed = rms_scale(local, moe_gain)
    positions = slot_positions(route_rows)
    select = (positions[None, :] == jnp.arange(E * CAP, dtype=jnp.int32)[:, None]).astype(
        jnp.bfloat16
    )
    repeated = jnp.repeat(normed, TOP, axis=0)
    table = jnp.dot(select, repeated, preferred_element_type=jnp.float32).astype(jnp.bfloat16)
    by_expert = table.reshape(E, CAP, width)
    first = lax.axis_index("seq") % 2 == 0
    outgoing = jnp.repeat(by_expert, 2, axis=0).reshape(seq_count, per_device, CAP, width)
    received = lax.all_to_all(outgoing, "seq", split_axis=0, concat_axis=0, tiled=True)
    projected = jnp.einsum("spcd,pdh->spch", received, gate_up, preferred_element_type=jnp.float32)
    gate_part = projected[..., :HALF]
    up_part = projected[..., HALF:]
    hidden = (gate_part * jax.nn.sigmoid(1.702 * gate_part) * (up_part + 1.0)).astype(jnp.bfloat16)
    partial_value = jnp.einsum(
        "spch,phd->spcd", hidden, down_proj, preferred_element_type=jnp.float32
    )
    if per_device >= 2:
        finished = (
            partial_value.reshape(seq_count, per_device // 2, 2, CAP, width)
            .sum(axis=2)
            .astype(jnp.bfloat16)
        )
    else:
        lower_rows = partial_value[:, :, : CAP // 2]
        upper_rows = partial_value[:, :, CAP // 2 :]
        kept = jnp.where(first, lower_rows, upper_rows)
        given = jnp.where(first, upper_rows, lower_rows)
        partner_part = from_partner(given.astype(jnp.bfloat16), "seq", 0).astype(given.dtype)
        finished = (kept + partner_part).astype(jnp.bfloat16)
    summed = lax.all_to_all(finished, "seq", split_axis=0, concat_axis=0, tiled=True).reshape(
        E * CAP, width
    )
    picked = lax.dot_general(
        select, summed, (((0,), (0,)), ((), ())), preferred_element_type=jnp.float32
    )
    weighted = jnp.sum(picked.reshape(tok_count, TOP, width) * route_scale[:, :, None], axis=1)
    return (local.astype(jnp.float32) + weighted).astype(jnp.bfloat16)


def attend(query_matrix, keys_extended, values_extended, head_sink_logits, halo_valid):
    tok_count = query_matrix.shape[0]
    query_groups = QUERY_HEADS // KEY_VALUE_HEADS
    attention_block = min(tok_count, 512)
    scale = float(HEAD_SIZE) ** (-0.5)
    sink_mass_total = jnp.exp(head_sink_logits).reshape(KEY_VALUE_HEADS, query_groups, 1, 1)
    block_queries = query_matrix.reshape(attention_block, KEY_VALUE_HEADS, query_groups, HEAD_SIZE)
    block_keys = keys_extended.reshape(attention_block + WINDOW_SPAN, KEY_VALUE_HEADS, HEAD_SIZE)
    block_values = values_extended.reshape(
        attention_block + WINDOW_SPAN, KEY_VALUE_HEADS, HEAD_SIZE
    )
    scores = (
        jnp.einsum("qhgd,khd->hgqk", block_queries, block_keys, preferred_element_type=jnp.float32)
        * scale
    )
    query_pos = jnp.arange(attention_block, dtype=jnp.int32)[:, None] + WINDOW_SPAN
    key_pos = jnp.arange(attention_block + WINDOW_SPAN, dtype=jnp.int32)[None, :]
    distance = query_pos - key_pos
    allowed = (
        (distance >= 0) & (distance < WINDOW_SPAN) & ((key_pos + 0 >= WINDOW_SPAN) | halo_valid)
    )
    weights = jnp.where(allowed, jnp.exp(scores), 0.0)
    probs = (weights / (jnp.sum(weights, axis=-1, keepdims=True) + sink_mass_total)).astype(
        jnp.bfloat16
    )
    mixed = jnp.einsum("hgqk,khd->qhgd", probs, block_values, preferred_element_type=jnp.float32)
    outputs = mixed.reshape(attention_block, QUERY_HEADS * HEAD_SIZE).astype(jnp.bfloat16)
    return outputs


def body(
    tokens,
    routes,
    route_weights,
    moe_gain,
    gate_up,
    down_proj,
    attn_gain,
    qkv_proj,
    head_sink_logits,
    out_proj,
):
    hidden = expert_layer(tokens[0], routes[0], route_weights[0], moe_gain, gate_up, down_proj)
    tok_count, width = hidden.shape
    normed = rms_scale(hidden, attn_gain)
    seq_index = lax.axis_index("seq")
    pipe_index = lax.axis_index("pipe")
    halo_valid = (seq_index > 0) | (pipe_index > 0)
    query_width = QUERY_HEADS * HEAD_SIZE
    width_of_pair = KEY_VALUE_HEADS * HEAD_SIZE
    columns = normed
    packed_heads = jnp.dot(
        columns,
        lax.all_gather(qkv_proj, "seq", axis=0, tiled=True),
        preferred_element_type=jnp.float32,
    ).astype(jnp.bfloat16)
    from_left = shifted(packed_heads[tok_count - WINDOW_SPAN :, query_width:], "seq", 1)
    from_section = passed_along(from_left, "pipe", 1)
    halo_pairs = jnp.where(seq_index == 0, from_section, from_left)
    query_matrix = packed_heads[:, :query_width]
    pairs_ext = jnp.concatenate([halo_pairs, packed_heads[:, query_width:]], axis=0)
    keys_extended = pairs_ext[:, :width_of_pair]
    values_extended = pairs_ext[:, width_of_pair:]
    attended = attend(query_matrix, keys_extended, values_extended, head_sink_logits, halo_valid)
    columns = attended
    projected = jnp.dot(
        columns,
        lax.all_gather(out_proj, "seq", axis=0, tiled=True),
        preferred_element_type=jnp.float32,
    )
    return (hidden.astype(jnp.float32) + projected).astype(jnp.bfloat16)[None]


def ring_place(index, count, folded):
    if not folded:
        return index
    line, side = index // 2, index % 2
    return line + side * (count - 1 - 2 * line)

def ring_index(place, count, folded):
    if not folded:
        return place
    side = place // (count // 2)
    line = place + side * (count - 1 - 2 * place)
    return 2 * line + side

def greet(peers):
    barrier = pltpu.get_barrier_semaphore()
    for peer in peers:
        pl.semaphore_signal(barrier, inc=1, device_id={"seq": peer}, device_id_type=MESH)
    pl.semaphore_wait(barrier, len(peers))

def remote(src, dst, send, recv, peer):
    return pltpu.make_async_remote_copy(src_ref=src, dst_ref=dst, send_sem=send, recv_sem=recv,
        device_id={"seq": peer}, device_id_type=MESH)

def gather_kernel(count, folded, own_ref, all_ref, send_sem, recv_sem):
    me = lax.axis_index("seq")
    place = ring_place(me, count, folded)
    at = lambda offset: ring_index(lax.rem(place + offset + count, count), count, folded)
    peers = (at(1), at(-1))
    greet(peers)
    rows = own_ref.shape[0]
    steps = count // 2
    copies = []
    for step in range(steps):
        for way in (0, 1):
            origin = at(-step if way == 0 else step)
            part = pl.ds(way * (rows // 2), rows // 2) if step == steps - 1 else pl.ds(0, rows)
            if step:
                copies[2 * (step - 1) + way].wait_recv()
            src = all_ref.at[origin, part] if step else own_ref.at[part]
            copy = remote(src, all_ref.at[origin, part], send_sem.at[way, step], recv_sem.at[way, step], peers[way])
            copy.start()
            copies.append(copy)
        if step == 0:
            all_ref[me] = own_ref[...]
    for copy in copies[-2:]:
        copy.wait_recv()
    for copy in copies:
        copy.wait_send()

def ring_gather(own, folded, cid):
    count = lax.axis_size("seq")
    steps = count // 2
    return pl.pallas_call(functools.partial(gather_kernel, count, folded),
        out_shape=jax.ShapeDtypeStruct((count,) + own.shape, own.dtype),
        in_specs=[pl.BlockSpec(memory_space=pltpu.VMEM)],
        out_specs=pl.BlockSpec(memory_space=pltpu.VMEM),
        scratch_shapes=[pltpu.SemaphoreType.DMA((2, steps)), pltpu.SemaphoreType.DMA((2, steps))],
        compiler_params=pltpu.CompilerParams(collective_id=cid, has_side_effects=True))(own)

def scatter_kernel(count, folded, part_ref, out_ref, held, send_sem, recv_sem):
    me = lax.axis_index("seq")
    place = ring_place(me, count, folded)
    at = lambda offset: ring_index(lax.rem(place + offset + count, count), count, folded)
    peers = (at(1), at(-1))
    greet(peers)
    rows = part_ref.shape[1]
    half = rows // 2
    steps = count // 2
    copies = []
    for step in range(steps):
        for way in (0, 1):
            goal = at((steps - step) * (1 if way == 0 else -1))
            whole = pl.ds(way * half, half) if step == 0 else pl.ds(0, rows)
            if step == 0:
                src = part_ref.at[goal, whole]
            else:
                copies[2 * (step - 1) + way].wait_recv()
                src = held.at[way, step - 1]
                if step == 1:
                    mine, other = pl.ds(way * half, half), pl.ds((1 - way) * half, half)
                    held[way, 0, mine] = (held[way, 0, mine].astype(jnp.float32) + part_ref[goal, mine].astype(jnp.float32)).astype(held.dtype)
                    held[way, 0, other] = part_ref[goal, other]
                else:
                    held[way, step - 1] = (held[way, step - 1].astype(jnp.float32) + part_ref[goal].astype(jnp.float32)).astype(held.dtype)
            copy = remote(src, held.at[way, step, whole], send_sem.at[way, step], recv_sem.at[way, step], peers[way])
            copy.start()
            copies.append(copy)
    for copy in copies[-2:]:
        copy.wait_recv()
    out_ref[...] = part_ref[me].astype(jnp.float32) + held[0, steps - 1].astype(jnp.float32) + held[1, steps - 1].astype(jnp.float32)
    for copy in copies:
        copy.wait_send()

def ring_scatter(parts, folded, cid):
    count = lax.axis_size("seq")
    steps = count // 2
    rows, width = parts.shape[1:]
    return pl.pallas_call(functools.partial(scatter_kernel, count, folded),
        out_shape=jax.ShapeDtypeStruct((rows, width), jnp.float32),
        in_specs=[pl.BlockSpec(memory_space=pltpu.VMEM)],
        out_specs=pl.BlockSpec(memory_space=pltpu.VMEM),
        scratch_shapes=[pltpu.VMEM((2, steps, rows, width), parts.dtype),
            pltpu.SemaphoreType.DMA((2, steps)), pltpu.SemaphoreType.DMA((2, steps))],
        compiler_params=pltpu.CompilerParams(collective_id=cid, has_side_effects=True, vmem_limit_bytes=40 << 20))(parts)


def exchanged(value):
    return lax.ppermute(value, "pipe", [(0, 1), (1, 0)])


def experts_by_rings(local, route_rows, route_scale, moe_gain, gate_up, down_proj, folded):
    tok_count, width = local.shape
    seq_count = lax.axis_size("seq")
    per_device = gate_up.shape[0]
    own_experts = per_device // 2
    normed = rms_scale(local, moe_gain)
    named = route_rows[:, :, None] == jnp.arange(E, dtype=jnp.int32)[None, None, :]
    dense = jnp.sum(jnp.where(named, route_scale[:, :, None], 0.0), axis=1).astype(jnp.bfloat16)
    filler = jnp.zeros((tok_count, -(width + E) % 128), jnp.bfloat16)
    gathered = ring_gather(jnp.concatenate([normed, dense, filler], axis=1), folded, 0)
    rows = gathered[:, :, :width]
    scales = lax.dynamic_slice_in_dim(
        gathered[:, :, width : width + E], lax.axis_index("seq") * own_experts, own_experts, axis=2
    ).transpose(0, 2, 1)
    present = scales > 0
    before = (
        jnp.arange(tok_count, dtype=jnp.int32)[:, None]
        < jnp.arange(tok_count, dtype=jnp.int32)[None, :]
    ).astype(jnp.bfloat16)
    earlier = jnp.einsum(
        "neu,ut->net", present.astype(jnp.bfloat16), before, preferred_element_type=jnp.float32
    ).astype(jnp.int32)
    slot = jnp.where(present, earlier, -1)
    taken = slot[:, :, None, :] == jnp.arange(CAP, dtype=jnp.int32)[None, None, :, None]
    select = jnp.repeat(taken.astype(jnp.bfloat16), 2, axis=1)
    received = jnp.einsum(
        "npct,ntd->npcd", select, rows, preferred_element_type=jnp.float32
    ).astype(jnp.bfloat16)
    projected = jnp.einsum("spcd,pdh->spch", received, gate_up, preferred_element_type=jnp.float32)
    half = projected.shape[-1] // 2
    gate_part = projected[..., :half]
    up_part = projected[..., half:]
    hidden = (gate_part * jax.nn.sigmoid(1.702 * gate_part) * (up_part + 1.0)).astype(jnp.bfloat16)
    partial_value = jnp.einsum(
        "spch,phd->spcd", hidden, down_proj, preferred_element_type=jnp.float32
    )
    finished = (
        partial_value.reshape(seq_count, own_experts, 2, CAP, width)
        .sum(axis=2)
        .astype(jnp.bfloat16)
        .reshape(seq_count, own_experts * CAP, width)
    )
    combine = jnp.where(taken, scales[:, :, None, :], 0).astype(jnp.bfloat16)
    parts = jnp.einsum(
        "nkt,nkd->ntd",
        combine.reshape(seq_count, own_experts * CAP, tok_count),
        finished,
        preferred_element_type=jnp.float32,
    ).astype(jnp.bfloat16)
    weighted = ring_scatter(parts, folded, 1)
    return (local.astype(jnp.float32) + weighted).astype(jnp.bfloat16)


def split_body(
    folded,
    tokens,
    routes,
    route_weights,
    moe_gain,
    gate_up,
    down_proj,
    attn_gain,
    qkv_proj,
    head_sink_logits,
    out_proj,
):
    seq_count = lax.axis_size("seq")
    seq_index = lax.axis_index("seq")
    pipe_index = lax.axis_index("pipe")
    query_width = QUERY_HEADS * HEAD_SIZE
    kv_width = KEY_VALUE_HEADS * HEAD_SIZE
    share = out_proj.shape[0] // 2
    own_heads = QUERY_HEADS // 2
    query_part = lax.dynamic_index_in_dim(
        qkv_proj[:, :query_width].reshape(qkv_proj.shape[0], seq_count, 2, share),
        pipe_index,
        axis=2,
        keepdims=False,
    ).reshape(qkv_proj.shape[0], query_width // 2)
    qkv_part = jnp.concatenate([query_part, qkv_proj[:, query_width:]], axis=1)
    out_part = lax.dynamic_slice_in_dim(out_proj, pipe_index * share, share, axis=0)
    qkv_whole = lax.all_gather(qkv_part, "seq", axis=0, tiled=True)
    out_whole = lax.all_gather(out_part, "seq", axis=0, tiled=True)
    sinks = lax.dynamic_index_in_dim(
        head_sink_logits.reshape(seq_count, 2, share // HEAD_SIZE),
        pipe_index,
        axis=1,
        keepdims=False,
    ).reshape(KEY_VALUE_HEADS, own_heads // KEY_VALUE_HEADS, 1, 1)

    hidden = experts_by_rings(
        tokens[0], routes[0], route_weights[0], moe_gain, gate_up, down_proj, folded
    )
    tok_count, width = hidden.shape
    normed = rms_scale(hidden, attn_gain)
    other = exchanged(normed)
    first = pipe_index == 0
    both = jnp.concatenate(
        [jnp.where(first, normed, other), jnp.where(first, other, normed)], axis=0
    )
    packed = jnp.dot(both, qkv_whole, preferred_element_type=jnp.float32).astype(jnp.bfloat16)
    packed = packed.reshape(2, tok_count, query_width // 2 + 2 * kv_width)
    pairs = packed[:, :, query_width // 2 :]
    from_left = shifted(pairs[:, tok_count - WINDOW_SPAN :], "seq", 1)
    halo = jnp.where(seq_index == 0, from_left[:1], from_left)
    extended = jnp.concatenate([halo, pairs], axis=1)
    keys = extended[:, :, :kv_width].reshape(2, -1, KEY_VALUE_HEADS, HEAD_SIZE)
    values = extended[:, :, kv_width:].reshape(2, -1, KEY_VALUE_HEADS, HEAD_SIZE)
    queries = packed[:, :, : query_width // 2].reshape(
        2, tok_count, KEY_VALUE_HEADS, own_heads // KEY_VALUE_HEADS, HEAD_SIZE
    )
    scores = jnp.einsum(
        "mqhgd,mkhd->mhgqk", queries, keys, preferred_element_type=jnp.float32
    ) * (float(HEAD_SIZE) ** (-0.5))
    query_pos = jnp.arange(tok_count, dtype=jnp.int32)[:, None] + WINDOW_SPAN
    key_pos = jnp.arange(tok_count + WINDOW_SPAN, dtype=jnp.int32)[None, :]
    distance = query_pos - key_pos
    inside = (distance >= 0) & (distance < WINDOW_SPAN)
    known = (jnp.arange(2, dtype=jnp.int32) > 0) | (seq_index > 0)
    allowed = inside[None] & ((key_pos >= WINDOW_SPAN)[None] | known[:, None, None])
    weights = jnp.where(allowed[:, None, None], jnp.exp(scores), 0.0)
    probs = (weights / (jnp.sum(weights, axis=-1, keepdims=True) + jnp.exp(sinks))).astype(
        jnp.bfloat16
    )
    mixed = jnp.einsum("mhgqk,mkhd->mqhgd", probs, values, preferred_element_type=jnp.float32)
    attended = mixed.astype(jnp.bfloat16).reshape(2 * tok_count, query_width // 2)
    projected = jnp.dot(attended, out_whole, preferred_element_type=jnp.float32)
    early, late = projected[:tok_count], projected[tok_count:]
    given = jnp.where(first, late, early).astype(jnp.bfloat16)
    kept = jnp.where(first, early, late)
    total = kept + exchanged(given).astype(jnp.float32)
    return (hidden.astype(jnp.float32) + total).astype(jnp.bfloat16)[None]


def solution(mesh):
    in_specs = (
        P("pipe", ("groups", "seq"), None),
        P("pipe", ("groups", "seq"), None),
        P("pipe", ("groups", "seq"), None),
        P(),
        P("seq", None, None),
        P("seq", None, None),
        P(),
        P("seq", None),
        P(),
        P("seq", None),
    )
    out_specs = P("pipe", ("groups", "seq"), None)
    seq_count, pipe_count = mesh.shape["seq"], mesh.shape["pipe"]
    split = (
        pipe_count == 2
        and seq_count % 2 == 0
        and 2 * E // seq_count >= 2
        and QUERY_HEADS % (2 * seq_count) == 0
    )
    chosen = functools.partial(split_body, True) if split else body
    return jax.shard_map(
        chosen, mesh=mesh, in_specs=in_specs, out_specs=out_specs, check_vma=False
    )
```
